512 devices in a mesh: ta: 8 (over x, y_lo), ha: 8 (over y_hi, core), wa: 8 (over z).
Axes of the slice: x: 4, y: 8 (y_hi: 4, y_lo: 2; y = y_hi * 2 + y_lo), z: 8, core: 2. Of those that a mesh axis runs over, the one named last changes fastest.
Arguments:
- queries: bfloat16 [24, 32, 64, 1536], P('ta', 'ha', 'wa'), may hold values from -6 to 6
- keys: bfloat16 [24, 32, 64, 1536], P('ta', 'ha', 'wa'), may hold values from -6 to 6
- values: bfloat16 [24, 32, 64, 1536], P('ta', 'ha', 'wa'), may hold values from -6 to 6
- radius: int32 [12, 3], replicated, may hold values from 0 to 1
- out_weight: bfloat16 [1536, 3072], P(('ha', 'wa')), may hold values from -0.15625 to 0.15625
Outputs:
- mixed_out: bfloat16 [24, 32, 64, 3072], P('ta', 'ha', 'wa')
The draws below stay inside these ranges and needn't reach their ends.
All inputs are finite; a program needn't handle non-finite values.
Results may differ from the reference program's by a relative error of at most 0.0057.
Values may be sent and summed in bfloat16 or wider, within the bound.
A program may use at most 128 MiB of HBM per device.

```python
import math
import jax
import jax.numpy as jnp
from jax import lax

D = 3072
HEADS = 12
HEAD_DIM = 128
TILE = 4
R = 1536
FRAMES = 24
HEIGHT = 32
WIDTH = 64


def draw_queries(key, part):
    shape = (FRAMES, HEIGHT, WIDTH, HEADS * HEAD_DIM)
    base = jnp.clip(jax.random.normal(jax.random.fold_in(key, 711), shape, jnp.float32), -6.0, 6.0)
    return base.astype(jnp.bfloat16)


def draw_keys(key, part):
    shape = (FRAMES, HEIGHT, WIDTH, HEADS * HEAD_DIM)
    base = jnp.clip(jax.random.normal(jax.random.fold_in(key, 721), shape, jnp.float32), -6.0, 6.0)
    return base.astype(jnp.bfloat16)


def set_ends(result, stream_key, least, top_value):
    longest = result.shape.index(max(result.shape))
    spots = []
    for shift in (0, 1):
        where = [jax.random.randint(jax.random.fold_in(stream_key, axis), (), 0, length) for axis, length in enumerate(result.shape)]
        where[longest] = (where[longest] + shift) % result.shape[longest]
        spots.append(tuple(where))
    return result.at[spots[0]].set(least).at[spots[1]].set(top_value)


def levels(own_key, shape, cuts, least, largest):
    def one(dim, parts):
        draws = jax.random.uniform(jax.random.fold_in(jax.random.fold_in(own_key, 6), dim), (parts,), jnp.float32, least / len(cuts), largest / len(cuts))
        return jnp.repeat(jnp.exp(draws), shape[dim] // parts).reshape((-1,) + (1,) * (len(shape) - dim - 1))

    loudness = one(*cuts[0])
    for cut in cuts[1:]:
        loudness = loudness * one(*cut)
    return loudness


def centred(rng, dims, scale, limit, shards=(), held_as=jnp.bfloat16):
    values = scale * jax.random.normal(rng, dims, jnp.float32)
    if shards:
        values = values * levels(rng, dims, shards, -0.22, 0.18)
    return jnp.clip(values, -limit, limit).astype(held_as)


def setup_inputs(seed: int = 0) -> dict:
    streams_of = jax.random.split(jax.random.key(seed), 6)
    queries = draw_queries(jax.random.fold_in(streams_of[5], 71), 0)
    keys = draw_keys(jax.random.fold_in(streams_of[5], 71), 0)
    values = centred(streams_of[2], (FRAMES, HEIGHT, WIDTH, R), 1.0, 6.0, ((0, 8), (1, 8), (2, 8)))
    radius = set_ends(jax.random.randint(streams_of[3], (HEADS, 3), 0, 2), jax.random.fold_in(streams_of[3], 1), 0, 1).astype(jnp.int32)
    out_weight = centred(streams_of[4], (R, D), R ** -0.5, 0.15625, ((0, 64),))
    return {"queries": queries, "keys": keys, "values": values, "radius": radius, "out_weight": out_weight}


def reference(queries, keys, values, radius, out_weight):
    frames, height, width_all, features = queries.shape
    head_count = radius.shape[0]
    head_dim = features // head_count
    tiles_h = height // TILE
    tiles_w = width_all // TILE
    pad_spec = ((1, 1), (TILE, TILE), (TILE, TILE), (0, 0))
    key_pad = jnp.pad(keys, pad_spec)
    value_pad = jnp.pad(values, pad_spec)
    inside = jnp.pad(jnp.ones((frames, height, width_all), jnp.float32), pad_spec[:3])
    shape_four = (3, 3 * TILE, 3, TILE)
    off_t = lax.broadcasted_iota(jnp.int32, shape_four, 0).reshape(-1) - 1
    off_h = lax.broadcasted_iota(jnp.int32, shape_four, 1).reshape(-1) // TILE - 1
    off_w = lax.broadcasted_iota(jnp.int32, shape_four, 2).reshape(-1) - 1
    allowed_head = (jnp.abs(off_t)[None, :] <= radius[:, 0:1]) & (jnp.abs(off_h)[None, :] <= radius[:, 1:2]) & (jnp.abs(off_w)[None, :] <= radius[:, 2:3])
    score_scale = 1.0 / math.sqrt(head_dim)

    def arrange(block):
        others = block.shape[3:]
        split = block.reshape((3, 3 * TILE, tiles_w + 2, TILE) + others)
        stacked = jnp.stack([split[:, :, offset:offset + tiles_w] for offset in range(3)], axis=2)
        moved = jnp.moveaxis(stacked, 3, 0)
        return moved.reshape((tiles_w, 27 * TILE * TILE) + others)

    def one_row(position):
        frame = position // tiles_h
        band = position % tiles_h
        anchor = jnp.int32(0)
        query_block = lax.dynamic_slice(queries, (frame, band * TILE, anchor, anchor), (1, TILE, width_all, features))
        query_tiles = query_block.reshape(TILE, tiles_w, TILE, head_count, head_dim).transpose(1, 0, 2, 3, 4).reshape(tiles_w, TILE * TILE, head_count, head_dim)
        corner = (frame, band * TILE, anchor, anchor)
        extent = (3, 3 * TILE, width_all + 2 * TILE, features)
        key_tiles = arrange(lax.dynamic_slice(key_pad, corner, extent)).reshape(tiles_w, -1, head_count, head_dim)
        value_tiles = arrange(lax.dynamic_slice(value_pad, corner, extent)).reshape(tiles_w, -1, head_count, head_dim)
        inside_tiles = arrange(lax.dynamic_slice(inside, (frame, band * TILE, anchor), (3, 3 * TILE, width_all + 2 * TILE)))
        allowed = allowed_head[None, :, None, :] & (inside_tiles[:, None, None, :] > 0.5)
        scores = jnp.einsum('jqhd,jkhd->jhqk', query_tiles.astype(jnp.float32), key_tiles.astype(jnp.float32), precision=lax.Precision.HIGHEST) * score_scale
        scores = jnp.where(allowed, scores, -jnp.inf)
        biggest = lax.optimization_barrier(jnp.max(scores, axis=-1, keepdims=True))
        expo = jnp.exp(scores - biggest)
        probs = (expo / lax.optimization_barrier(jnp.sum(expo, axis=-1, keepdims=True))).astype(jnp.bfloat16)
        attended = jnp.einsum('jhqk,jkhd->jqhd', probs.astype(jnp.float32), value_tiles.astype(jnp.float32), precision=lax.Precision.HIGHEST).astype(jnp.bfloat16)
        return attended.reshape(tiles_w, TILE, TILE, features).transpose(1, 0, 2, 3).reshape(TILE, width_all, features)
    bands = lax.map(one_row, jnp.arange(frames * tiles_h, dtype=jnp.int32))
    attended = bands.reshape(frames * height * width_all, features)
    mixed_out = jnp.dot(attended, out_weight, preferred_element_type=jnp.float32).astype(jnp.bfloat16)
    return mixed_out.reshape(frames, height, width_all, out_weight.shape[1])
```

```python
import math

import jax
import jax.numpy as jnp
from jax import lax
from jax.experimental import pallas as pl
from jax.experimental.pallas import tpu as pltpu
from jax.sharding import PartitionSpec as P

D = 3072
TILE = 4
HEADS = 12
HEAD_DIM = 128
R = HEADS * HEAD_DIM
CHUNKS = 4
PER_CHUNK = HEADS // CHUNKS
NA = 8
FRAMES_HERE = 3
TOKENS = 96
ROWS_W = 24
HALF = D // 2
PIECE = D // 4
COLS = 512
MESH = pl.DeviceIdType.MESH


def kernel(q_ref, k_ref, v_ref, rad_ref, w_ref, o_ref, kv, wbuf, code, att, send_sems, recv_sems, local_sem):
    ta, ha, wa = lax.axis_index("ta"), lax.axis_index("ha"), lax.axis_index("wa")
    core = lax.rem(ha, 2)
    par = lax.rem(lax.div(ta, 2), 2)

    def step(pos, by):
        return lax.rem(pos + (by + NA), NA)

    partner = ha + 1 - 2 * core

    barrier = pltpu.get_barrier_semaphore()
    greet = [{"ta": step(ta, d)} for d in (1, -1, 2, -2)]
    greet += [{"ha": step(ha, d)} for d in range(1, NA)]
    greet += [{"wa": step(wa, d)} for d in (1, -1)]
    for who in greet:
        pl.semaphore_signal(barrier, inc=1, device_id=who, device_id_type=MESH)

    to = lax.broadcasted_iota(jnp.int32, (TOKENS, TOKENS), 0)
    come = lax.broadcasted_iota(jnp.int32, (TOKENS, TOKENS), 1)
    frame, left = to // 32, to % 32
    source = frame * 32 + ((left % 16) // 4) * 8 + (left // 16) * 4 + left % 4
    order = (source == come).astype(jnp.bfloat16)
    for which, ref in ((0, k_ref), (1, v_ref)):
        moved = jnp.dot(order, ref[...], preferred_element_type=jnp.float32).astype(jnp.bfloat16)
        for head in range(HEADS):
            part = moved[:, head * HEAD_DIM : (head + 1) * HEAD_DIM]
            kv[head, which, 1:4, 1, 1:3] = part.reshape(FRAMES_HERE, 2, 16, HEAD_DIM)

    pl.semaphore_wait(barrier, len(greet))

    started = []

    def send(src, dst, who):
        i = len(started)
        copy = pltpu.make_async_remote_copy(
            src_ref=src, dst_ref=dst, send_sem=send_sems.at[i], recv_sem=recv_sems.at[i],
            device_id=who, device_id_type=MESH,
        )
        copy.start()
        started.append(copy)
        return copy

    def piece(parity, which_core):
        return pl.ds(pl.multiple_of(which_core * HALF + parity * PIECE, 128), PIECE)

    mine = piece(par, core)

    def heads_of(c):
        return pl.ds(c * PER_CHUNK, PER_CHUNK)

    own = pltpu.make_async_copy(w_ref.at[:, mine], wbuf.at[ha, wa, :, mine], local_sem)
    own.start()

    def send_t(c):
        h = heads_of(c)
        return [
            send(kv.at[h, :, 3, 1, 1:3], kv.at[h, :, 0, 1, 1:3], {"ta": step(ta, 1)}),
            send(kv.at[h, :, 1, 1, 1:3], kv.at[h, :, 4, 1, 1:3], {"ta": step(ta, -1)}),
        ]

    t_copies = [send_t(0)]
    y_copies = []
    for d in range(1, NA):
        other = step(ha, d)
        cols = piece(par, lax.rem(other, 2))
        y_copies.append(send(w_ref.at[:, cols], wbuf.at[ha, wa, :, cols], {"ha": other}))
    t_copies += [send_t(c) for c in range(1, CHUNKS)]

    def send_h(c):
        for copy in t_copies[c]:
            copy.wait_recv()
        h = heads_of(c)
        return [
            send(kv.at[h, :, :, 1, 1:3], kv.at[h, :, :, 0, 1:3], {"ha": step(ha, 1)}),
            send(kv.at[h, :, :, 1, 1:3], kv.at[h, :, :, 2, 1:3], {"ha": step(ha, -1)}),
        ]

    def send_w(c):
        for copy in h_copies[c]:
            copy.wait_recv()
        h = heads_of(c)
        rows = pl.ds(core, 2)
        return [
            send(kv.at[h, :, :, rows, 2], kv.at[h, :, :, rows, 0], {"wa": step(wa, 1)}),
            send(kv.at[h, :, :, rows, 1], kv.at[h, :, :, rows, 3], {"wa": step(wa, -1)}),
        ]

    def send_c(c):
        for copy in w_copies[c]:
            copy.wait_recv()
        h = heads_of(c)
        there = 2 * core
        return [
            send(kv.at[h, :, :, 1, 0], kv.at[h, :, :, there, 0], {"ha": partner}),
            send(kv.at[h, :, :, 1, 3], kv.at[h, :, :, there, 3], {"ha": partner}),
        ]

    def ring_up(r):
        at = step(wa, 1 - r)
        return send(wbuf.at[:, at, :, mine], wbuf.at[:, at, :, mine], {"wa": step(wa, 1)})

    def ring_down(r):
        at = step(wa, r - 1)
        return send(wbuf.at[:, at, :, mine], wbuf.at[:, at, :, mine], {"wa": step(wa, -1)})

    def send_x(at):
        return [
            send(wbuf.at[4:8, at, :, mine], wbuf.at[4:8, at, :, mine], {"ta": step(ta, 2)}),
            send(wbuf.at[0:4, at, :, mine], wbuf.at[0:4, at, :, mine], {"ta": step(ta, -2)}),
        ]

    def send_pair(block):
        at, copies = block
        for copy in copies:
            copy.wait_recv()
        cols = pl.ds(pl.multiple_of(core * HALF, 128), HALF)
        return send(wbuf.at[:, at, :, cols], wbuf.at[:, at, :, cols], {"ha": partner})

    def attend(c):
        for copy in c_copies[c]:
            copy.wait_recv()

        @pl.loop(0, PER_CHUNK)
        def _(i):
            head = c * PER_CHUNK + i
            lanes = pl.ds(pl.multiple_of(head * HEAD_DIM, 128), HEAD_DIM)
            closed = 8
            for axis in range(3):
                closed = closed + jnp.where(rad_ref[head, axis] == 0, 1 << axis, 0)
            for f in range(FRAMES_HERE):
                q = q_ref[f * 32 : (f + 1) * 32, lanes]
                k = kv[head, 0, f : f + 3].reshape(576, HEAD_DIM)
                v = kv[head, 1, f : f + 3].reshape(576, HEAD_DIM)
                s = lax.dot_general(q, k, (((1,), (1,)), ((), ())), preferred_element_type=jnp.float32)
                s = s * (1.0 / math.sqrt(HEAD_DIM))
                s = jnp.where((code[f] & closed) == 0, s, -jnp.inf)
                biggest = jnp.max(s, axis=-1, keepdims=True)
                expo = jnp.exp(s - biggest)
                probs = (expo / jnp.sum(expo, axis=-1, keepdims=True)).astype(jnp.bfloat16)
                out = jnp.dot(probs, v, preferred_element_type=jnp.float32)
                att[f * 32 : (f + 1) * 32, lanes] = out.astype(jnp.bfloat16)

    qi = lax.broadcasted_iota(jnp.int32, (32, 576), 0)
    kj = lax.broadcasted_iota(jnp.int32, (32, 576), 1)
    dt = kj // 192 - 1
    dh = (kj % 192) // 64 - 1
    wj = (kj % 64) // 16
    dw = jnp.abs(wj - 1 - (qi % 8) // 4)
    row_at, col_at = ha + dh, 2 * wa + wj - 1
    never = (dw > 1) | (row_at < 0) | (row_at >= NA) | (col_at < 0) | (col_at >= 2 * NA)
    kind = jnp.where(dt == 0, 0, 1) + jnp.where(dh == 0, 0, 2) + jnp.where(dw == 0, 0, 4)
    for f in range(FRAMES_HERE):
        frame_at = FRAMES_HERE * ta + f + dt
        out_of = never | (frame_at < 0) | (frame_at >= FRAMES_HERE * NA)
        code[f] = kind + jnp.where(out_of, 8, 0)

    h_copies = [send_h(0)]
    own.wait()
    for copy in y_copies:
        copy.wait_recv()
    blocks = []
    up, down = [ring_up(1)], [ring_down(1)]
    blocks.append((wa, send_x(wa)))
    h_copies.append(send_h(1))
    h_copies.append(send_h(2))
    h_copies.append(send_h(3))

    w_copies, c_copies, pair_copies = [], [], []

    def next_ring(r):
        up[-1].wait_recv()
        if r < 4:
            up.append(ring_up(r + 1))
        blocks.append((step(wa, -r), send_x(step(wa, -r))))
        if r < 4:
            down[-1].wait_recv()
            if r < 3:
                down.append(ring_down(r + 1))
            blocks.append((step(wa, r), send_x(step(wa, r))))

    w_copies.append(send_w(0))
    next_ring(1)
    w_copies.append(send_w(1))
    c_copies.append(send_c(0))
    next_ring(2)
    w_copies.append(send_w(2))
    c_copies.append(send_c(1))
    attend(0)
    next_ring(3)
    w_copies.append(send_w(3))
    pair_copies.append(send_pair(blocks[0]))
    c_copies.append(send_c(2))
    attend(1)
    next_ring(4)
    pair_copies.append(send_pair(blocks[1]))
    pair_copies.append(send_pair(blocks[2]))
    c_copies.append(send_c(3))
    attend(2)
    pair_copies.append(send_pair(blocks[3]))
    pair_copies.append(send_pair(blocks[4]))
    attend(3)
    for block in blocks[5:]:
        pair_copies.append(send_pair(block))

    def project(which_core):
        @pl.loop(0, HALF // COLS)
        def _(n):
            cols = pl.ds(pl.multiple_of(which_core * HALF + n * COLS, 128), COLS)
            w = wbuf[:, :, :, cols].reshape(R, COLS)
            o_ref[:, cols] = jnp.dot(att[...], w, preferred_element_type=jnp.float32).astype(jnp.bfloat16)

    project(core)
    for copy in pair_copies:
        copy.wait_recv()
    project(1 - core)
    for copy in started:
        copy.wait_send()


COPIES = 8 * CHUNKS + 7 + 7 + 16 + 8


def shards(queries, keys, values, radius, out_weight):
    shape = queries.shape[:3]
    vmem = pl.BlockSpec(memory_space=pltpu.VMEM)
    out = pl.pallas_call(
        kernel,
        out_shape=jax.ShapeDtypeStruct((TOKENS, D), jnp.bfloat16),
        in_specs=[vmem, vmem, vmem, pl.BlockSpec(memory_space=pltpu.SMEM), vmem],
        out_specs=vmem,
        scratch_shapes=[
            pltpu.VMEM((HEADS, 2, 5, 3, 4, 16, HEAD_DIM), jnp.bfloat16),
            pltpu.VMEM((NA, NA, ROWS_W, D), jnp.bfloat16),
            pltpu.VMEM((FRAMES_HERE, 32, 576), jnp.int32),
            pltpu.VMEM((TOKENS, R), jnp.bfloat16),
            pltpu.SemaphoreType.DMA((COPIES,)),
            pltpu.SemaphoreType.DMA((COPIES,)),
            pltpu.SemaphoreType.DMA,
        ],
        compiler_params=pltpu.CompilerParams(
            collective_id=0, has_side_effects=True, vmem_limit_bytes=48 * 1024 * 1024
        ),
    )(
        queries.reshape(TOKENS, R),
        keys.reshape(TOKENS, R),
        values.reshape(TOKENS, R),
        radius,
        out_weight,
    )
    return out.reshape(*shape, D)


def solution(mesh):
    return jax.shard_map(
        shards,
        mesh=mesh,
        in_specs=(
            P("ta", "ha", "wa", None),
            P("ta", "ha", "wa", None),
            P("ta", "ha", "wa", None),
            P(),
            P(("ha", "wa"), None),
        ),
        out_specs=P("ta", "ha", "wa", None),
        check_vma=False,
    )
```

```python
import math

import jax
import jax.numpy as jnp
from jax import lax
from jax.experimental import pallas as pl
from jax.experimental.pallas import tpu as pltpu
from jax.sharding import PartitionSpec as P

D = 3072
TILE = 4
HEADS = 12
HEAD_DIM = 128
R = HEADS * HEAD_DIM
CHUNKS = ((0, 4), (4, 3), (7, 3), (10, 2))
NA = 8
FRAMES_HERE = 3
TOKENS = 96
ROWS_W = 24
HALF = D // 2
PIECE = D // 4
COLS = 512
COPIES = 96
MESH = pl.DeviceIdType.MESH


def kernel(
    q_hbm, k_hbm, v_hbm, rad_ref, w_hbm, o_ref,
    q_ref, k_ref, v_ref, w_ref, kv, wbuf, code, att, send_sems, recv_sems, local_sems,
):
    loads = [
        pltpu.make_async_copy(src, dst, local_sems.at[i])
        for i, (src, dst) in enumerate(((k_hbm, k_ref), (v_hbm, v_ref), (w_hbm, w_ref), (q_hbm, q_ref)))
    ]
    for load in loads:
        load.start()

    ta, ha, wa = lax.axis_index("ta"), lax.axis_index("ha"), lax.axis_index("wa")
    core = lax.rem(ha, 2)
    par = lax.rem(lax.div(ta, 2), 2)

    def step(pos, by):
        return lax.rem(pos + (by + NA), NA)

    partner = ha + 1 - 2 * core
    outer = 2 * core

    other_core = {"ha": partner}
    odd = lax.rem(ta, 2)
    twin = ta + 1 - 2 * odd
    away = 2 * odd - 1

    def chip_at(by, e):
        return lax.rem(lax.div(ha, 2) + by + NA, NA // 2) * 2 + lax.rem(core + e, 2)

    barrier = pltpu.get_barrier_semaphore()
    greet = [{"ta": step(ta, d)} for d in (1, -1, 2, -2)]
    greet += [{"wa": step(wa, d)} for d in (1, -1)]
    greet += [other_core]
    greet += [{"ha": chip_at(by, e)} for by in (1, -1) for e in (0, 1)]
    greet += [{"ta": twin, "ha": chip_at(by * away, e)} for by in (1, 2) for e in (0, 1)]
    for who in greet:
        pl.semaphore_signal(barrier, inc=1, device_id=who, device_id_type=MESH)

    to = lax.broadcasted_iota(jnp.int32, (TOKENS, TOKENS), 0)
    come = lax.broadcasted_iota(jnp.int32, (TOKENS, TOKENS), 1)
    frame, left = to // 32, to % 32
    source = frame * 32 + ((left % 16) // 4) * 8 + (left // 16) * 4 + left % 4
    order = (source == come).astype(jnp.bfloat16)
    for which, ref in ((0, k_ref), (1, v_ref)):
        loads[which].wait()
        moved = jnp.dot(order, ref[...], preferred_element_type=jnp.float32).astype(jnp.bfloat16)
        for head in range(HEADS):
            part = moved[:, head * HEAD_DIM : (head + 1) * HEAD_DIM]
            kv[head, which, 1:4, 1, 1:3] = part.reshape(FRAMES_HERE, 2, 16, HEAD_DIM)
    loads[2].wait()

    pl.semaphore_wait(barrier, len(greet))

    started = []

    def send(src, dst, who):
        i = len(started)
        copy = pltpu.make_async_remote_copy(
            src_ref=src, dst_ref=dst, send_sem=send_sems.at[i], recv_sem=recv_sems.at[i],
            device_id=who, device_id_type=MESH,
        )
        copy.start()
        started.append(copy)
        return copy

    def arrived(copies):
        for copy in copies:
            copy.wait_recv()

    def piece(parity, which_core):
        return pl.ds(pl.multiple_of(which_core * HALF + parity * PIECE, 128), PIECE)

    mine = piece(par, core)
    ta_up, ta_down = {"ta": step(ta, 1)}, {"ta": step(ta, -1)}
    ha_up, ha_down = {"ha": step(ha, 1)}, {"ha": step(ha, -1)}
    wa_up, wa_down = {"wa": step(wa, 1)}, {"wa": step(wa, -1)}

    y_copies = []
    for where in ({"ta": twin, "ha": 1}, {"ta": ta, "ha": 1}, {"ta": twin, "ha": 2}):
        for e in (0, 1):
            there = {"ta": where["ta"], "ha": chip_at(where["ha"] * away, e)}
            cols = piece(par, lax.rem(core + e, 2))
            y_copies.append(send(w_ref.at[:, cols], wbuf.at[ha, wa, :, cols], there))
    cols = piece(par, 1 - core)
    y_copies.append(send(w_ref.at[:, cols], wbuf.at[ha, wa, :, cols], other_core))
    own = pltpu.make_async_copy(w_ref.at[:, mine], wbuf.at[ha, wa, :, mine], local_sems.at[4])
    own.start()

    def rim(frames):
        return [
            send(kv.at[:, :, frames, 1, 2], kv.at[:, :, frames, 1, 0], wa_up),
            send(kv.at[:, :, frames, 1, 1], kv.at[:, :, frames, 1, 3], wa_down),
        ]

    def rim_across(frames):
        return [
            send(kv.at[:, :, frames, 1, 0], kv.at[:, :, frames, outer, 0], other_core),
            send(kv.at[:, :, frames, 1, 3], kv.at[:, :, frames, outer, 3], other_core),
        ]

    def rows(c, frames):
        first, count = CHUNKS[c]
        src = kv.at[pl.ds(first, count), :, frames, 1, 1:3]
        return [
            send(src, kv.at[pl.ds(first, count), :, frames, 0, 1:3], ha_up),
            send(src, kv.at[pl.ds(first, count), :, frames, 2, 1:3], ha_down),
        ]

    def outer_rim(c):
        arrived(h_copies[c])
        heads = pl.ds(CHUNKS[c][0], CHUNKS[c][1])
        return [
            send(kv.at[heads, :, :, outer, 2], kv.at[heads, :, :, outer, 0], wa_up),
            send(kv.at[heads, :, :, outer, 1], kv.at[heads, :, :, outer, 3], wa_down),
        ]

    OWN = slice(1, 4)
    w_own = rim(OWN)
    t_copies = [
        send(kv.at[:, :, 3, 1, 1:3], kv.at[:, :, 0, 1, 1:3], ta_up),
        send(kv.at[:, :, 1, 1, 1:3], kv.at[:, :, 4, 1, 1:3], ta_down),
    ]
    h_copies = [rows(0, OWN)]

    qi = lax.broadcasted_iota(jnp.int32, (TOKENS, 960), 0)
    kj = lax.broadcasted_iota(jnp.int32, (TOKENS, 960), 1)
    dt = jnp.abs(kj // 192 - 1 - qi // 32)
    dh = (kj % 192) // 64 - 1
    wj = (kj % 64) // 16
    dw = jnp.abs(wj - 1 - (qi % 8) // 4)
    row_at, col_at = ha + dh, 2 * wa + wj - 1
    frame_at = FRAMES_HERE * ta + kj // 192 - 1
    never = (dw > 1) | (dt > 1) | (row_at < 0) | (row_at >= NA) | (col_at < 0) | (col_at >= 2 * NA)
    never = never | (frame_at < 0) | (frame_at >= FRAMES_HERE * NA)
    kind = jnp.where(dt == 0, 0, 1) + jnp.where(dh == 0, 0, 2) + jnp.where(dw == 0, 0, 4)
    code[...] = kind + jnp.where(never, 8, 0)

    x_copies, pair_copies = {}, []

    def block(half, at, cols):
        return wbuf.at[4 * half : 4 * half + 4, at, :, cols]

    def ring(half, way, r):
        at = step(wa, way * (1 - r))
        return send(block(half, at, mine), block(half, at, mine), wa_up if way == 1 else wa_down)

    def across_x(half, at, key):
        x_copies[key, half] = at, send(
            block(half, at, mine), block(half, at, mine), {"ta": step(ta, 2 if half else -2)}
        )

    def to_partner(key, half):
        at, copy = x_copies[key, half]
        copy.wait_recv()
        cols = pl.ds(pl.multiple_of(core * HALF, 128), HALF)
        pair_copies.append(send(block(half, at, cols), block(half, at, cols), other_core))

    own.wait()
    arrived(y_copies)
    rings = {}
    for half in (0, 1):
        for way in (1, -1):
            rings[half, way, 1] = ring(half, way, 1)
        across_x(half, wa, 0)

    def next_ring(r, halves=(0, 1)):
        for half in halves:
            for way in (1, -1):
                if (half, way, r) not in rings:
                    continue
                rings[half, way, r].wait_recv()
                if r < 3 or (r == 3 and way == 1 - 2 * half):
                    rings[half, way, r + 1] = ring(half, way, r + 1)
                across_x(half, step(wa, -way * r), way * r if r < 4 else 4)

    def attend(c):
        arrived(o_copies[c])

        @pl.loop(0, CHUNKS[c][1])
        def _(i):
            head = CHUNKS[c][0] + i
            lanes = pl.ds(pl.multiple_of(head * HEAD_DIM, 128), HEAD_DIM)
            closed = 8
            for axis in range(3):
                closed = closed + jnp.where(rad_ref[axis, head] == 0, 1 << axis, 0)
            k = kv[head, 0].reshape(960, HEAD_DIM)
            v = kv[head, 1].reshape(960, HEAD_DIM)
            s = lax.dot_general(q_ref[:, lanes], k, (((1,), (1,)), ((), ())), preferred_element_type=jnp.float32)
            s = s * (1.0 / math.sqrt(HEAD_DIM))
            s = jnp.where((code[...] & closed) == 0, s, -jnp.inf)
            biggest = jnp.max(s, axis=-1, keepdims=True)
            expo = jnp.exp(s - biggest)
            probs = (expo * (1.0 / jnp.sum(expo, axis=-1, keepdims=True))).astype(jnp.bfloat16)
            out = jnp.dot(probs, v, preferred_element_type=jnp.float32)
            att[:, lanes] = out.astype(jnp.bfloat16)

    ALL = slice(0, 5)
    arrived(w_own)
    c_copies = rim_across(OWN)
    next_ring(1, (0,))
    arrived(t_copies)
    h_copies[0] = h_copies[0] + rows(0, 0) + rows(0, 4)
    h_copies += [rows(c, ALL) for c in range(1, len(CHUNKS))]
    w_t = [rim(0), rim(4)]
    next_ring(1, (1,))
    next_ring(2)
    o_copies = [outer_rim(0)]
    for copies, f in zip(w_t, (0, 4)):
        arrived(copies)
        c_copies += rim_across(f)
    to_partner(0, 0)
    to_partner(0, 1)
    next_ring(3, (0,))
    o_copies.append(outer_rim(1))
    next_ring(3, (1,))
    loads[3].wait()
    arrived(c_copies)
    o_copies.append(outer_rim(2))
    for key in (1, -1):
        to_partner(key, 0)
        to_partner(key, 1)
    next_ring(4)
    o_copies.append(outer_rim(3))
    attend(0)
    for key in (2, -2):
        to_partner(key, 0)
        to_partner(key, 1)
    attend(1)
    for key in (3, -3, 4):
        to_partner(key, 0)
        to_partner(key, 1)
    attend(2)
    attend(3)

    def project(which_core):
        @pl.loop(0, HALF // COLS)
        def _(n):
            cols = pl.ds(pl.multiple_of(which_core * HALF + n * COLS, 128), COLS)
            w = wbuf[:, :, :, cols].reshape(R, COLS)
            o_ref[:, cols] = jnp.dot(att[...], w, preferred_element_type=jnp.float32).astype(jnp.bfloat16)

    project(core)
    arrived(pair_copies)
    project(1 - core)
    for copy in started:
        copy.wait_send()


def shards(queries, keys, values, radius, out_weight):
    shape = queries.shape[:3]
    hbm = pl.BlockSpec(memory_space=pltpu.HBM)
    out = pl.pallas_call(
        kernel,
        out_shape=jax.ShapeDtypeStruct((TOKENS, D), jnp.bfloat16),
        in_specs=[hbm, hbm, hbm, pl.BlockSpec(memory_space=pltpu.SMEM), hbm],
        out_specs=pl.BlockSpec(memory_space=pltpu.VMEM),
        scratch_shapes=[
            pltpu.VMEM((TOKENS, R), jnp.bfloat16),
            pltpu.VMEM((TOKENS, R), jnp.bfloat16),
            pltpu.VMEM((TOKENS, R), jnp.bfloat16),
            pltpu.VMEM((ROWS_W, D), jnp.bfloat16),
            pltpu.VMEM((HEADS, 2, 5, 3, 4, 16, HEAD_DIM), jnp.bfloat16),
            pltpu.VMEM((NA, NA, ROWS_W, D), jnp.bfloat16),
            pltpu.VMEM((TOKENS, 960), jnp.int32),
            pltpu.VMEM((TOKENS, R), jnp.bfloat16),
            pltpu.SemaphoreType.DMA((COPIES,)),
            pltpu.SemaphoreType.DMA((COPIES,)),
            pltpu.SemaphoreType.DMA((5,)),
        ],
        compiler_params=pltpu.CompilerParams(
            collective_id=0, has_side_effects=True, vmem_limit_bytes=67043328
        ),
    )(
        queries.reshape(TOKENS, R),
        keys.reshape(TOKENS, R),
        values.reshape(TOKENS, R),
        radius.T,
        out_weight,
    )
    return out.reshape(*shape, D)


def solution(mesh):
    return jax.shard_map(
        shards,
        mesh=mesh,
        in_specs=(
            P("ta", "ha", "wa", None),
            P("ta", "ha", "wa", None),
            P("ta", "ha", "wa", None),
            P(),
            P(("ha", "wa"), None),
        ),
        out_specs=P("ta", "ha", "wa", None),
        check_vma=False,
    )
```

```python
import math

import jax
import jax.numpy as jnp
from jax import lax
from jax.experimental import pallas as pl
from jax.experimental.pallas import tpu as pltpu
from jax.sharding import PartitionSpec as P

D = 3072
TILE = 4
HEADS = 12
HEAD_DIM = 128
R = HEADS * HEAD_DIM
CHUNKS = ((0, 3), (3, 4), (7, 3), (10, 2))
OVER_WA = 2
NA = 8
FRAMES_HERE = 3
TOKENS = 96
ROWS_W = 24
HALF = D // 2
PIECE = D // 4
COLS = 512
COPIES = 136
MESH = pl.DeviceIdType.MESH


def kernel(
    q_hbm, k_hbm, v_hbm, rad_ref, w_hbm, o_ref,
    q_ref, k_ref, v_ref, w_ref, kv, wbuf, code, att, send_sems, recv_sems, local_sems,
):
    loads = [
        pltpu.make_async_copy(src, dst, local_sems.at[i])
        for i, (src, dst) in enumerate(((k_hbm, k_ref), (v_hbm, v_ref), (w_hbm, w_ref), (q_hbm, q_ref)))
    ]
    for load in loads:
        load.start()

    ta, ha, wa = lax.axis_index("ta"), lax.axis_index("ha"), lax.axis_index("wa")
    core = lax.rem(ha, 2)
    par = lax.rem(lax.div(ta, 2), 2)

    def step(pos, by):
        return lax.rem(pos + (by + NA), NA)

    partner = ha + 1 - 2 * core
    outer = 2 * core

    other_core = {"ha": partner}
    odd = lax.rem(ta, 2)
    twin = ta + 1 - 2 * odd
    away = 2 * odd - 1

    def chip_at(by, e):
        return lax.rem(lax.div(ha, 2) + by + NA, NA // 2) * 2 + lax.rem(core + e, 2)

    barrier = pltpu.get_barrier_semaphore()
    greet = [{"ta": step(ta, d)} for d in (1, -1, 2, -2)]
    greet += [{"wa": step(wa, d)} for d in (1, -1)]
    greet += [other_core]
    greet += [{"ha": chip_at(by, e)} for by in (1, -1) for e in (0, 1)]
    greet += [{"ta": twin, "ha": chip_at(by * away, e)} for by in (1, 2) for e in (0, 1)]
    for who in greet:
        pl.semaphore_signal(barrier, inc=1, device_id=who, device_id_type=MESH)

    to = lax.broadcasted_iota(jnp.int32, (TOKENS, TOKENS), 0)
    come = lax.broadcasted_iota(jnp.int32, (TOKENS, TOKENS), 1)
    frame, left = to // 32, to % 32
    source = frame * 32 + ((left % 16) // 4) * 8 + (left // 16) * 4 + left % 4
    order = (source == come).astype(jnp.bfloat16)
    for which, ref in ((0, k_ref), (1, v_ref)):
        loads[which].wait()
        moved = jnp.dot(order, ref[...], preferred_element_type=jnp.float32).astype(jnp.bfloat16)
        for head in range(HEADS):
            part = moved[:, head * HEAD_DIM : (head + 1) * HEAD_DIM]
            kv[head, which, 1:4, 1, 1:3] = part.reshape(FRAMES_HERE, 2, 16, HEAD_DIM)
    loads[2].wait()

    pl.semaphore_wait(barrier, len(greet))

    started, shared = [], []

    def send(src, dst, who):
        i = len(started)
        copy = pltpu.make_async_remote_copy(
            src_ref=src, dst_ref=dst, send_sem=send_sems.at[i], recv_sem=recv_sems.at[i],
            device_id=who, device_id_type=MESH,
        )
        copy.start()
        started.append(copy)
        return copy

    def arrived(copies):
        for copy in copies:
            copy.wait_recv()

    def piece(parity, which_core):
        return pl.ds(pl.multiple_of(which_core * HALF + parity * PIECE, 128), PIECE)

    mine = piece(par, core)
    ta_up, ta_down = {"ta": step(ta, 1)}, {"ta": step(ta, -1)}
    ha_up, ha_down = {"ha": step(ha, 1)}, {"ha": step(ha, -1)}
    wa_up, wa_down = {"wa": step(wa, 1)}, {"wa": step(wa, -1)}

    own = pltpu.make_async_copy(w_ref.at[:, mine], wbuf.at[ha, wa, :, mine], local_sems.at[4])
    own.start()

    cols = piece(par, 1 - core)
    y_copies = [send(w_ref.at[:, cols], wbuf.at[ha, wa, :, cols], other_core)]
    for where in ({"ta": twin, "ha": 1}, {"ta": ta, "ha": 1}, {"ta": twin, "ha": 2}):
        for e in (0, 1):
            there = {"ta": where["ta"], "ha": chip_at(where["ha"] * away, e)}
            cols = piece(par, lax.rem(core + e, 2))
            y_copies.append(send(w_ref.at[:, cols], wbuf.at[ha, wa, :, cols], there))

    def rim(frames):
        return [
            send(kv.at[:, :, frames, 1, 2], kv.at[:, :, frames, 1, 0], wa_up),
            send(kv.at[:, :, frames, 1, 1], kv.at[:, :, frames, 1, 3], wa_down),
        ]

    def rim_across(frames):
        return [
            send(kv.at[:, :, frames, 1, 0], kv.at[:, :, frames, outer, 0], other_core),
            send(kv.at[:, :, frames, 1, 3], kv.at[:, :, frames, outer, 3], other_core),
        ]

    facing = 2 - outer
    beyond = step(ha, outer - 1)
    three, two, twin_two = pl.ds(2 * odd, 3), pl.ds(3 - 3 * odd, 2), pl.ds(3 * odd, 2)

    def heads_of(c):
        return pl.ds(CHUNKS[c][0], CHUNKS[c][1])

    def rows_inside(c, frames):
        heads = heads_of(c)
        return [send(kv.at[heads, :, frames, 1, 1:3], kv.at[heads, :, frames, outer, 1:3], other_core)]

    def rows_outside(c, frames):
        heads = heads_of(c)
        return [send(kv.at[heads, :, frames, 1, 1:3], kv.at[heads, :, frames, facing, 1:3], {"ha": beyond})]

    def rows_shared(c, cols):
        heads = heads_of(c)
        copies = [send(kv.at[heads, :, three, 1, cols], kv.at[heads, :, three, facing, cols], {"ha": beyond})]
        i = len(started)
        both = [
            pltpu.make_async_remote_copy(
                src_ref=kv.at[heads, :, two, 1, cols], dst_ref=kv.at[heads, :, at, facing, cols],
                send_sem=send_sems.at[i + k], recv_sem=recv_sems.at[i],
                device_id=where, device_id_type=MESH,
            )
            for k, (at, where) in enumerate(
                ((twin_two, {"ta": twin, "ha": beyond}), (two, {"ta": ta, "ha": beyond}))
            )
        ]

        @pl.when(odd == core)
        def _():
            for copy in both:
                copy.start()

        started.extend([None, None])
        shared.extend(both)
        return copies + [both[1]]

    def outer_rim(c):
        arrived(h_copies[c])
        heads = heads_of(c)
        return [
            send(kv.at[heads, :, :, outer, 2], kv.at[heads, :, :, outer, 0], wa_up),
            send(kv.at[heads, :, :, outer, 1], kv.at[heads, :, :, outer, 3], wa_down),
        ]

    OWN, ALL = slice(1, 4), slice(0, 5)
    t_copies = [
        send(kv.at[:, :, 3, 1, 1:3], kv.at[:, :, 0, 1, 1:3], ta_up),
        send(kv.at[:, :, 1, 1, 1:3], kv.at[:, :, 4, 1, 1:3], ta_down),
    ]
    h_copies = [rows_outside(0, OWN) + rows_inside(0, OWN)]

    x_copies, pair_copies, rings = {}, [], {}
    UNITS = (0, 1, 2, 3)

    def unit(u, at, cols):
        chip = lax.rem(lax.div(ha, 2) + (0, away, -away, 2)[u] + NA, NA // 2)
        return wbuf.at[pl.ds(2 * chip, 2), at, :, cols]

    def ring(u, way, r):
        at = step(wa, way * (1 - r))
        return send(unit(u, at, mine), unit(u, at, mine), wa_up if way == 1 else wa_down)

    def across_x(u, at, key):
        x_copies[key, u] = at, send(unit(u, at, mine), unit(u, at, mine), {"ta": step(ta, 2 if u % 2 else -2)})

    def to_partner(key):
        for u in UNITS:
            at, copy = x_copies[key, u]
            copy.wait_recv()
            cols = pl.ds(pl.multiple_of(core * HALF, 128), HALF)
            pair_copies.append(send(unit(u, at, cols), unit(u, at, cols), other_core))

    def first_ring(u):
        arrived(y_copies[:1] if u == 0 else y_copies[2 * u - 1 : 2 * u + 1])
        for way in (1, -1):
            rings[u, way, 1] = ring(u, way, 1)
        across_x(u, wa, 0)

    def next_ring(r, units=UNITS):
        for u in units:
            for way in (1, -1):
                if (u, way, r) not in rings:
                    continue
                rings[u, way, r].wait_recv()
                if r < 3 or (r == 3 and way == (-1 if u // 2 else 1)):
                    rings[u, way, r + 1] = ring(u, way, r + 1)
                across_x(u, step(wa, -way * r), way * r if r < 4 else 4)

    own.wait()
    first_ring(0)
    w_own = rim(OWN)

    qi = lax.broadcasted_iota(jnp.int32, (TOKENS, 960), 0)
    kj = lax.broadcasted_iota(jnp.int32, (TOKENS, 960), 1)
    dt = jnp.abs(kj // 192 - 1 - qi // 32)
    dh = (kj % 192) // 64 - 1
    wj = (kj % 64) // 16
    dw = jnp.abs(wj - 1 - (qi % 8) // 4)
    row_at, col_at = ha + dh, 2 * wa + wj - 1
    frame_at = FRAMES_HERE * ta + kj // 192 - 1
    never = (dw > 1) | (dt > 1) | (row_at < 0) | (row_at >= NA) | (col_at < 0) | (col_at >= 2 * NA)
    never = never | (frame_at < 0) | (frame_at >= FRAMES_HERE * NA)
    kind = jnp.where(dt == 0, 0, 1) + jnp.where(dh == 0, 0, 2) + jnp.where(dw == 0, 0, 4)
    code[...] = kind + jnp.where(never, 8, 0)

    for u in (1, 2, 3):
        first_ring(u)

    def attend(c):
        arrived(o_copies[c])

        @pl.loop(0, CHUNKS[c][1])
        def _(i):
            head = CHUNKS[c][0] + i
            lanes = pl.ds(pl.multiple_of(head * HEAD_DIM, 128), HEAD_DIM)
            closed = 8
            for axis in range(3):
                closed = closed + jnp.where(rad_ref[axis, head] == 0, 1 << axis, 0)
            k = kv[head, 0].reshape(960, HEAD_DIM)
            v = kv[head, 1].reshape(960, HEAD_DIM)
            s = lax.dot_general(q_ref[:, lanes], k, (((1,), (1,)), ((), ())), preferred_element_type=jnp.float32)
            s = s * (1.0 / math.sqrt(HEAD_DIM))
            s = jnp.where((code[...] & closed) == 0, s, -jnp.inf)
            biggest = jnp.max(s, axis=-1, keepdims=True)
            expo = jnp.exp(s - biggest)
            probs = (expo * (1.0 / jnp.sum(expo, axis=-1, keepdims=True))).astype(jnp.bfloat16)
            out = jnp.dot(probs, v, preferred_element_type=jnp.float32)
            att[:, lanes] = out.astype(jnp.bfloat16)

    arrived(w_own)
    c_copies = rim_across(OWN)
    next_ring(1, (0,))
    arrived(t_copies)
    w_t = [rim(0), rim(4)]
    for f in (0, 4):
        h_copies[0] = h_copies[0] + rows_outside(0, f) + rows_inside(0, f)
    h_copies += [rows_shared(c, slice(1, 3)) for c in range(1, OVER_WA)]
    for c in range(1, OVER_WA):
        h_copies[c] = h_copies[c] + rows_inside(c, ALL)
    next_ring(1, (1, 2, 3))
    for copies, f in zip(w_t, (0, 4)):
        arrived(copies)
        c_copies += rim_across(f)
    for c in range(OVER_WA, len(CHUNKS)):
        h_copies.append(rows_shared(c, slice(0, 4)) + rows_inside(c, ALL))
    next_ring(2)
    o_copies = [outer_rim(0)]
    to_partner(0)
    next_ring(3, (0, 1))
    o_copies += [outer_rim(c) for c in range(1, OVER_WA)]
    o_copies += h_copies[OVER_WA:]
    next_ring(3, (2, 3))
    loads[3].wait()
    arrived(c_copies)
    for key in (1, -1):
        to_partner(key)
    next_ring(4)
    attend(0)
    for key in (2, -2):
        to_partner(key)
    attend(1)
    for key in (3, -3, 4):
        to_partner(key)
    attend(2)
    attend(3)

    def project(which_core):
        @pl.loop(0, HALF // COLS)
        def _(n):
            cols = pl.ds(pl.multiple_of(which_core * HALF + n * COLS, 128), COLS)
            w = wbuf[:, :, :, cols].reshape(R, COLS)
            o_ref[:, cols] = jnp.dot(att[...], w, preferred_element_type=jnp.float32).astype(jnp.bfloat16)

    project(core)
    arrived(pair_copies)
    project(1 - core)
    for copy in started:
        if copy is not None:
            copy.wait_send()

    @pl.when(odd == core)
    def _():
        for copy in shared:
            copy.wait_send()


def shards(queries, keys, values, radius, out_weight):
    shape = queries.shape[:3]
    hbm = pl.BlockSpec(memory_space=pltpu.HBM)
    out = pl.pallas_call(
        kernel,
        out_shape=jax.ShapeDtypeStruct((TOKENS, D), jnp.bfloat16),
        in_specs=[hbm, hbm, hbm, pl.BlockSpec(memory_space=pltpu.SMEM), hbm],
        out_specs=pl.BlockSpec(memory_space=pltpu.VMEM),
        scratch_shapes=[
            pltpu.VMEM((TOKENS, R), jnp.bfloat16),
            pltpu.VMEM((TOKENS, R), jnp.bfloat16),
            pltpu.VMEM((TOKENS, R), jnp.bfloat16),
            pltpu.VMEM((ROWS_W, D), jnp.bfloat16),
            pltpu.VMEM((HEADS, 2, 5, 3, 4, 16, HEAD_DIM), jnp.bfloat16),
            pltpu.VMEM((NA, NA, ROWS_W, D), jnp.bfloat16),
            pltpu.VMEM((TOKENS, 960), jnp.int32),
            pltpu.VMEM((TOKENS, R), jnp.bfloat16),
            pltpu.SemaphoreType.DMA((COPIES,)),
            pltpu.SemaphoreType.DMA((COPIES,)),
            pltpu.SemaphoreType.DMA((5,)),
        ],
        compiler_params=pltpu.CompilerParams(
            collective_id=0, has_side_effects=True, vmem_limit_bytes=67043328
        ),
    )(
        queries.reshape(TOKENS, R),
        keys.reshape(TOKENS, R),
        values.reshape(TOKENS, R),
        radius.T,
        out_weight,
    )
    return out.reshape(*shape, D)


def solution(mesh):
    return jax.shard_map(
        shards,
        mesh=mesh,
        in_specs=(
            P("ta", "ha", "wa", None),
            P("ta", "ha", "wa", None),
            P("ta", "ha", "wa", None),
            P(),
            P(("ha", "wa"), None),
        ),
        out_specs=P("ta", "ha", "wa", None),
        check_vma=False,
    )
```
